32 devices in a mesh: dp: 2 (over x), row: 4 (over y, core), col: 4 (over z).
Axes of the slice: x: 2, y: 2, z: 4, core: 2. Of those that a mesh axis runs over, the one named last changes fastest.
Arguments:
- inputs: bfloat16 [14568, 12, 128], P(('dp', 'row'), 'col'), may hold values from -15 to 15
- mixer_weight: float32 [768, 2304], P('row', 'col'), may hold values from -0.3125 to 0.3125
- mixer_bias: float32 [12, 128], P('col', 'row'), may hold values from -3 to 3
- merge_weight: float32 [768, 768], P(('col', 'row')), may hold values from -0.875 to 0.875
- merge_bias: float32 [12, 64], P('col', 'row'), may hold values from -3 to 3
- expand_weight: float32 [768, 3072], P('row', 'col'), may hold values from -0.21875 to 0.21875
- expand_bias: float32 [12, 256], P('col', 'row'), may hold values from -3 to 3
- reduce_weight: float32 [3072, 768], P(('col', 'row')), may hold values from -0.109375 to 0.109375
- reduce_bias: float32 [12, 64], P('col', 'row'), may hold values from -3 to 3
- first_gain: float32 [12, 64], P('col', 'row'), may hold values from 0.1 to 1.9
- first_shift: float32 [12, 64], P('col', 'row'), may hold values from -3 to 3
- second_gain: float32 [12, 64], P('col', 'row'), may hold values from 0.1 to 1.9
- second_shift: float32 [12, 64], P('col', 'row'), may hold values from -3 to 3
- cotangent: bfloat16 [14568, 12, 128], P(('dp', 'row'), 'col'), may hold values from -6 to 6
Outputs:
- outputs: bfloat16 [14568, 12, 128], P(('dp', 'row'), 'col')
- input_grad: float32 [14568, 12, 128], P(('dp', 'row'), 'col')
- grad_mixer_weight: float32 [768, 2304], P('row', 'col')
- grad_mixer_bias: float32 [12, 128], P('col', 'row')
- grad_merge_weight: float32 [768, 768], P(('col', 'row'))
- grad_merge_bias: float32 [12, 64], P('col', 'row')
- grad_expand_weight: float32 [768, 3072], P('row', 'col')
- grad_expand_bias: float32 [12, 256], P('col', 'row')
- grad_reduce_weight: float32 [3072, 768], P(('col', 'row'))
- grad_reduce_bias: float32 [12, 64], P('col', 'row')
- grad_first_gain: float32 [12, 64], P('col', 'row')
- grad_first_shift: float32 [12, 64], P('col', 'row')
- grad_second_gain: float32 [12, 64], P('col', 'row')
- grad_second_shift: float32 [12, 64], P('col', 'row')
The draws below stay inside these ranges and needn't reach their ends.
All inputs are finite; a program needn't handle non-finite values.
Results may differ from the reference program's by a relative error of at most 0.012.
The reference program's roundings to bfloat16 on the way count: a program that leaves them out, or rounds other values in their place, can miss the bound.
Values may be sent and summed in bfloat16 or wider, within the bound.
A program may use at most 192 MiB of HBM per device.

```python
import jax
import jax.numpy as jnp
from jax import lax

D = 768
H = 12
HD = 64
FF = 3072
LEN = 1214
CLIPS_DEV = 3
CLIPS = 24
TOKENS = 29136


def draw_inputs(key, part):
    first = jax.random.fold_in(key, 0)
    ramp = 1.0 + 2.0 * jnp.arange(D, dtype=jnp.float32) / D
    base = jnp.clip(jax.random.normal(first, (TOKENS, D), jnp.float32), -5.0, 5.0)
    values = base * ramp[None, :]
    return values.reshape(TOKENS // 2, 2, H, HD).transpose(0, 2, 1, 3).reshape(TOKENS // 2, H, 2 * HD).astype(jnp.bfloat16)


def levels(key, extent, cuts, low, top_value):
    def one(dim, blocks):
        draws = jax.random.uniform(jax.random.fold_in(jax.random.fold_in(key, 6), dim), (blocks,), jnp.float32, low / len(cuts), top_value / len(cuts))
        return jnp.repeat(jnp.exp(draws), extent[dim] // blocks).reshape((-1,) + (1,) * (len(extent) - dim - 1))

    level = one(*cuts[0])
    for cut in cuts[1:]:
        level = level * one(*cut)
    return level


def normal_values(key, shape, scale, limit, cuts=(), held_as=jnp.bfloat16):
    values = scale * jax.random.normal(key, shape, jnp.float32)
    if cuts:
        values = values * levels(key, shape, cuts, -0.22, 0.18)
    return jnp.clip(values, -limit, limit).astype(held_as)


def setup_inputs(seed: int = 0) -> dict:
    seeds = jax.random.split(jax.random.key(seed), 15)
    return {
        "inputs": draw_inputs(jax.random.fold_in(seeds[14], 71), 0),
        "mixer_weight": normal_values(seeds[1], (D, 3 * D), (D // 2) ** -0.5, 0.3125, ((0, 4), (1, 4)), jnp.float32),
        "mixer_bias": normal_values(seeds[2], (H, 2 * HD), 0.5, 3.0, ((0, 4), (1, 4)), jnp.float32),
        "merge_weight": normal_values(seeds[3], (D, D), (D // 16) ** -0.5, 0.875, ((0, 16),), jnp.float32),
        "merge_bias": normal_values(seeds[4], (H, HD), 0.5, 3.0, ((0, 4), (1, 4)), jnp.float32),
        "expand_weight": normal_values(seeds[5], (D, FF), D ** -0.5, 0.21875, ((0, 4), (1, 4)), jnp.float32),
        "expand_bias": normal_values(seeds[6], (H, FF // H), 0.5, 3.0, ((0, 4), (1, 4)), jnp.float32),
        "reduce_weight": normal_values(seeds[7], (FF, D), FF ** -0.5, 0.109375, ((0, 16),), jnp.float32),
        "reduce_bias": normal_values(seeds[8], (H, HD), 0.5, 3.0, ((0, 4), (1, 4)), jnp.float32),
        "first_gain": jnp.clip(1.0 + 0.18 * jax.random.normal(seeds[9], (H, HD), jnp.float32), 0.1, 1.9),
        "first_shift": normal_values(seeds[10], (H, HD), 0.5, 3.0, ((0, 4), (1, 4)), jnp.float32),
        "second_gain": jnp.clip(1.0 + 0.18 * jax.random.normal(seeds[11], (H, HD), jnp.float32), 0.1, 1.9),
        "second_shift": normal_values(seeds[12], (H, HD), 0.5, 3.0, ((0, 4), (1, 4)), jnp.float32),
        "cotangent": normal_values(seeds[13], (TOKENS // 2, H, 2 * HD), 1.0, 6.0, ((0, 8), (1, 4))),
    }


@jax.custom_vjp
def low(v):
    return lax.optimization_barrier(v.astype(jnp.bfloat16)).astype(jnp.float32)

@jax.custom_vjp
def low_back(v):
    return v

def low_keep(v):
    return (low(v), None)

def low_pass(kept, grad):
    return (grad,)

def back_keep(v):
    return (v, None)

def back_low(kept, grad):
    return (low(grad),)
low.defvjp(low_keep, low_pass)
low_back.defvjp(back_keep, back_low)
EPSILON = 1e-06
HIGHEST = lax.Precision.HIGHEST

def to_rows(values):
    halves = values.shape[0]
    return values.reshape(halves, H, 2, HD).transpose(0, 2, 1, 3).reshape(2 * halves, D)

def from_rows(values):
    halves = values.shape[0] // 2
    return values.reshape(halves, 2, H, HD).transpose(0, 2, 1, 3).reshape(halves, H, 2 * HD)

def layer_norm(values, gain, shift):
    centre = lax.optimization_barrier(jnp.mean(values, axis=-1, keepdims=True))
    centered = values - centre
    spread = lax.optimization_barrier(jnp.mean(centered * centered, axis=-1, keepdims=True))
    return centered * lax.rsqrt(spread + EPSILON) * gain + shift

def attend_block(parts):
    query, keyset, valueset = parts
    scores = low_back(jnp.dot(query, keyset.T, precision=HIGHEST) * HD ** (-0.5))
    chances = jax.nn.softmax(scores, axis=-1)
    return jnp.dot(low(chances), valueset, precision=HIGHEST)

def exact_gelu(values):
    return jax.nn.gelu(values, approximate=False)

def forward(params, rows):
    rounded = tuple((low(param) for param in params))
    mixer_mat, mixer_vec, merge_mat, merge_vec, expand_mat, expand_vec, reduce_mat, reduce_vec, gain_one, shift_one, gain_two, shift_two = rounded
    count = rows.shape[0]
    clips = count // LEN
    normed = low(layer_norm(rows, gain_one.reshape(D), shift_one.reshape(D)))
    pairs = mixer_vec.reshape(H, 2, HD)
    full_bias = jnp.stack([pairs[:, 0], jnp.zeros_like(pairs[:, 0]), pairs[:, 1]], axis=1).reshape(3 * D)
    mixed = jnp.dot(normed, mixer_mat, precision=HIGHEST) + full_bias
    mixed = low_back(low(mixed))
    mixed = mixed.reshape(clips, LEN, H, 3, HD).transpose(3, 0, 2, 1, 4).reshape(3, clips * H, LEN, HD)
    heads = lax.map(jax.checkpoint(attend_block), (mixed[0], mixed[1], mixed[2]))
    heads = heads.reshape(clips, H, LEN, HD).transpose(0, 2, 1, 3).reshape(count, D)
    heads = low_back(low(heads))
    branch = jnp.dot(heads, merge_mat, precision=HIGHEST) + merge_vec.reshape(D)
    state = rows + low_back(branch)
    normed_two = low(layer_norm(state, gain_two.reshape(D), shift_two.reshape(D)))
    hidden = low_back(jnp.dot(normed_two, expand_mat, precision=HIGHEST) + expand_vec.reshape(FF))
    active = low(exact_gelu(hidden))
    return state + jnp.dot(active, reduce_mat, precision=HIGHEST) + reduce_vec.reshape(D)

def add_pair(left, right):
    return left + right

def reference(inputs, mixer_weight, mixer_bias, merge_weight, merge_bias, expand_weight, expand_bias, reduce_weight, reduce_bias, first_gain, first_shift, second_gain, second_shift, cotangent):
    params = (mixer_weight, mixer_bias, merge_weight, merge_bias, expand_weight, expand_bias, reduce_weight, reduce_bias, first_gain, first_shift, second_gain, second_shift)
    blocks = CLIPS // CLIPS_DEV
    rows = to_rows(inputs.astype(jnp.float32)).reshape(blocks, CLIPS_DEV * LEN, D)
    cotans = to_rows(cotangent.astype(jnp.float32)).reshape(blocks, CLIPS_DEV * LEN, D)

    def one_block(totals, pair):
        block, cotan = pair
        result, pull = jax.vjp(forward, params, block)
        grads, back = pull(cotan)
        totals = jax.tree.map(add_pair, totals, grads)
        return (totals, (result.astype(jnp.bfloat16), back))
    zeros = jax.tree.map(jnp.zeros_like, params)
    totals, (results, backs) = lax.scan(one_block, zeros, (rows, cotans))
    return (from_rows(results.reshape(TOKENS, D)), from_rows(backs.reshape(TOKENS, D)), totals[0], totals[1], totals[2], totals[3], totals[4], totals[5], totals[6], totals[7], totals[8], totals[9], totals[10], totals[11])
```

```python
import functools

import jax
import jax.numpy as jnp
from jax import lax
from jax.experimental import pallas as pl
from jax.experimental.pallas import tpu as pltpu
from jax.sharding import PartitionSpec as P

D = 768
HD = 64
LEN = 1214
EPSILON = 1e-06
PAIRS = LEN // 2
TILE = 152
ROWS = 2 * TILE
KEYS = 4 * ROWS
WIDE = 640
BLOCK = 304
NT = (((1,), (1,)), ((), ()))
TN = (((0,), (0,)), ((), ()))
NN = (((1,), (0,)), ((), ()))
f32 = jnp.float32
bf16 = jnp.bfloat16
PLANE = ("row", "col")
BLOCKS = ("col", "row")


def dot(left, right, dims=NN):
    return lax.dot_general(left, right, dims, preferred_element_type=f32)


HEADS = ((0, 1, 2, 0, 0), (0, 1, 2, 1, 1), (3, 4, 3, 0, 1))
ORDER = ((0, 0), (1, 0), (0, 1), (1, 1), (0, 2), (1, 2), (2, 0), (2, 2), (2, 1))


def widen(values):
    pieces = [values[..., (3 * h + s) * HD : (3 * h + s + 1) * HD] for h, s in ORDER]
    pieces.append(jnp.zeros_like(pieces[0]))
    return jnp.concatenate(pieces, axis=-1)


def narrow(values):
    place = {pair: at for at, pair in enumerate(ORDER)}
    pieces = []
    for h in range(3):
        for s in range(3):
            at = place[(h, s)]
            pieces.append(values[..., at * HD : (at + 1) * HD])
    return jnp.concatenate(pieces, axis=-1)


def key_bias():
    index = lax.broadcasted_iota(jnp.int32, (1, KEYS), 1)
    padded = (index == KEYS - 1 - TILE) | (index == KEYS - 1)
    return jnp.where(padded, -1e30, 0.0).astype(f32)


def tile(ref, at):
    return ref[0, :, 128 * at : 128 * at + 128]


def attend_kernel(mixed_ref, out_ref, sum_ref):
    bias = key_bias()
    lane = lax.broadcasted_iota(jnp.int32, (1, 128), 1)
    low = lane < HD

    def block(step, carry):
        rows = pl.ds(pl.multiple_of(step * BLOCK, 8), BLOCK)
        outs = []
        sums = []
        for qt, kt, vt, qh, vh in HEADS:
            query = mixed_ref[0, rows, 128 * qt : 128 * qt + 128]
            query = jnp.where(low == (qh == 0), query, jnp.zeros_like(query))
            query = query * jnp.asarray(0.125, bf16)
            scores = dot(query, tile(mixed_ref, kt), NT) + bias
            highest = jnp.max(scores, axis=1, keepdims=True)
            weights = jnp.exp(scores - highest)
            total = jnp.sum(weights, axis=1, keepdims=True)
            outs.append(dot(weights.astype(bf16), tile(mixed_ref, vt)) * (1.0 / total))
            sums.append(highest + jnp.log(total))
        out_ref[0, rows, 0:128] = jnp.where(low, outs[0], outs[1]).astype(bf16)
        out_ref[0, rows, 128:256] = jnp.where(low, 0.0, outs[2]).astype(bf16)
        sum_ref[0, rows, :] = jnp.where(lane == 0, sums[0], jnp.where(lane == 1, sums[1], sums[2]))
        return carry

    lax.fori_loop(0, KEYS // BLOCK, block, 0)


def attend(mixed):
    slots = mixed.shape[0]
    return pl.pallas_call(
        attend_kernel,
        grid=(slots,),
        in_specs=[pl.BlockSpec((1, KEYS, WIDE), lambda i: (i, 0, 0))],
        out_specs=[
            pl.BlockSpec((1, KEYS, 256), lambda i: (i, 0, 0)),
            pl.BlockSpec((1, KEYS, 128), lambda i: (i, 0, 0)),
        ],
        out_shape=[
            jax.ShapeDtypeStruct((slots, KEYS, 256), bf16),
            jax.ShapeDtypeStruct((slots, KEYS, 128), f32),
        ],
        cost_estimate=pl.CostEstimate(
            flops=12 * slots * KEYS * KEYS * 128,
            bytes_accessed=slots * KEYS * 2 * (WIDE + 512),
            transcendentals=3 * slots * KEYS * KEYS,
        ),
        name="attend",
    )(mixed)


def attend_back_kernel(mixed_ref, grad_ref, sum_ref, out_ref, key_sum, value_sum):
    bias = key_bias()
    lane = lax.broadcasted_iota(jnp.int32, (1, 128), 1)
    low = lane < HD
    key_sum[...] = jnp.zeros_like(key_sum)
    value_sum[...] = jnp.zeros_like(value_sum)

    def block(step, carry):
        rows = pl.ds(pl.multiple_of(step * BLOCK, 8), BLOCK)
        sums = sum_ref[0, rows, :]
        queries = []
        for head, (qt, kt, vt, qh, vh) in enumerate(HEADS):
            query = mixed_ref[0, rows, 128 * qt : 128 * qt + 128]
            query = jnp.where(low == (qh == 0), query, jnp.zeros_like(query))
            query = query * jnp.asarray(0.125, bf16)
            at = head // 2
            grad = grad_ref[0, rows, 128 * at : 128 * at + 128]
            grad = jnp.where(low == (vh == 0), grad, jnp.zeros_like(grad))
            scores = dot(query, tile(mixed_ref, kt), NT) + bias
            chances = jnp.exp(scores - sums[:, head : head + 1])
            grad_chances = dot(grad, tile(mixed_ref, vt), NT)
            inner = jnp.sum(grad_chances * chances, axis=1, keepdims=True)
            grad_scores = (chances * (grad_chances - inner)).astype(bf16)
            value_sum[at] += dot(chances.astype(bf16), grad, TN)
            key_sum[at] += dot(grad_scores, query, TN)
            queries.append(dot(grad_scores, tile(mixed_ref, kt)) * 0.125)
        out_ref[0, rows, 0:128] = jnp.where(low, queries[0], queries[1]).astype(bf16)
        out_ref[0, rows, 384:512] = jnp.where(low, queries[2], 0.0).astype(bf16)
        return carry

    lax.fori_loop(0, KEYS // BLOCK, block, 0)
    out_ref[0, :, 128:256] = key_sum[0].astype(bf16)
    out_ref[0, :, 256:384] = value_sum[0].astype(bf16)
    out_ref[0, :, 384:512] = jnp.where(low, out_ref[0, :, 384:512], value_sum[1].astype(bf16))
    out_ref[0, :, 512:640] = key_sum[1].astype(bf16)


def attend_back(mixed, grads, sums):
    slots = mixed.shape[0]
    return pl.pallas_call(
        attend_back_kernel,
        grid=(slots,),
        in_specs=[
            pl.BlockSpec((1, KEYS, WIDE), lambda i: (i, 0, 0)),
            pl.BlockSpec((1, KEYS, 256), lambda i: (i, 0, 0)),
            pl.BlockSpec((1, KEYS, 128), lambda i: (i, 0, 0)),
        ],
        out_specs=pl.BlockSpec((1, KEYS, WIDE), lambda i: (i, 0, 0)),
        out_shape=jax.ShapeDtypeStruct((slots, KEYS, WIDE), bf16),
        scratch_shapes=[pltpu.VMEM((2, KEYS, 128), f32), pltpu.VMEM((2, KEYS, 128), f32)],
        cost_estimate=pl.CostEstimate(
            flops=30 * slots * KEYS * KEYS * 128,
            bytes_accessed=slots * KEYS * 2 * (2 * WIDE + 512),
            transcendentals=3 * slots * KEYS * KEYS,
        ),
        name="attend_back",
    )(mixed, grads, sums)


def plane_index(row, col):
    return 4 * row + col


def spread_pairs(step):
    pairs = []
    for half in range(2):
        for bit in range(2):
            for col in range(4):
                member = col ^ step
                pairs.append(
                    (
                        plane_index(2 * half + bit, col),
                        plane_index(2 * half + member // 2, 2 * bit + member % 2),
                    )
                )
    return pairs


def take(values, index):
    return lax.dynamic_index_in_dim(values, index, 0, keepdims=False)


def to_members(values, col, member):
    width = values.shape[1] * values.shape[2]
    clips = values.reshape(-1, PAIRS, width)
    last = jnp.pad(clips[:, 3 * TILE :], ((0, 0), (0, 4 * TILE - PAIRS), (0, 0)))
    blocks = jnp.concatenate([clips[:, : 3 * TILE], last.reshape(1, 3 * TILE, width)])
    got = jnp.stack(
        [lax.ppermute(take(blocks, col ^ step), PLANE, spread_pairs(step)) for step in range(4)]
    )
    whole = jnp.concatenate([take(got, source ^ member) for source in range(4)], axis=1)
    heads = 4 * values.shape[1]
    return (
        whole.reshape(3, TILE, heads, 2, HD)
        .transpose(0, 3, 1, 2, 4)
        .reshape(3 * ROWS, heads * HD)
    )


def from_members(values, col, member):
    heads = values.shape[1] // HD
    width = values.shape[1] * 2 // 4
    whole = values.reshape(3, 2, TILE, heads, HD).transpose(0, 2, 3, 1, 4)
    parts = whole.reshape(3 * TILE, 4, width).transpose(1, 0, 2)
    got = jnp.stack(
        [
            lax.ppermute(
                take(parts, member ^ step),
                PLANE,
                [(target, source) for source, target in spread_pairs(step)],
            )
            for step in range(4)
        ]
    )
    blocks = jnp.stack([take(got, col ^ other) for other in range(4)])
    last = blocks[3].reshape(3, TILE, width)[:, : PAIRS - 3 * TILE]
    clips = jnp.concatenate([blocks[:3], last], axis=1)
    return clips.reshape(3 * PAIRS, width // 128, 128)


def swap_pairs(member):
    pairs = []
    for half in range(2):
        for pair in range(2):
            one = plane_index(2 * half + member // 2, 2 * pair + member % 2)
            other = plane_index(2 * half + 1, 2 * pair + 1)
            pairs += [(one, other), (other, one)]
    return pairs


def to_slots(values, last):
    got = [
        lax.ppermute(jnp.where(last, values[:3, at], values[3]), PLANE, swap_pairs(at))
        for at in range(3)
    ]
    mine = got[0] + got[1] + got[2]
    head = jnp.where(last, jnp.stack(got), values[:3])
    tail = jnp.where(last, values[3], mine)
    return jnp.concatenate([head, tail[:, None]], axis=1)


def from_slots(values, last):
    got = [
        lax.ppermute(jnp.where(last, values[at, :3], values[:, 3]), PLANE, swap_pairs(at))
        for at in range(3)
    ]
    mine = got[0] + got[1] + got[2]
    head = jnp.where(last, jnp.stack(got, axis=1), values[:, :3])
    tail = jnp.where(last, values[:, 3], mine)
    return jnp.concatenate([head, tail[None]])


def norm(values, gain, shift):
    centre = jnp.mean(values, axis=1, keepdims=True)
    centered = values - centre
    spread = jnp.mean(centered * centered, axis=1, keepdims=True)
    inverse = lax.rsqrt(spread + EPSILON)
    scaled = centered * inverse
    return (scaled * gain + shift, scaled, inverse)


def norm_back(grads, scaled, inverse, gain):
    upstream = grads * gain
    first = jnp.mean(upstream, axis=1, keepdims=True)
    second = jnp.mean(upstream * scaled, axis=1, keepdims=True)
    result = inverse * (upstream - first - scaled * second)
    return (result, jnp.sum(grads * scaled, axis=0), jnp.sum(grads, axis=0))


def many(left, right, left_dims, right_dims, left_batch=(), right_batch=()):
    return lax.dot_general(
        left,
        right,
        ((left_dims, right_dims), (left_batch, right_batch)),
        preferred_element_type=f32,
    )


def gelu_parts(values):
    chance = 0.5 * (1.0 + lax.erf(values * (0.5**0.5)))
    density = jnp.exp(-0.5 * values * values) * (0.5 / jnp.pi) ** 0.5
    return (values * chance, chance + values * density)


def body(
    inputs,
    mixer_weight,
    mixer_bias,
    merge_weight,
    merge_bias,
    expand_weight,
    expand_bias,
    reduce_weight,
    reduce_bias,
    first_gain,
    first_shift,
    second_gain,
    second_shift,
    cotangent,
):
    row = lax.axis_index("row")
    col = lax.axis_index("col")
    member = 2 * (row % 2) + col % 2
    last = member == 3

    small = (
        mixer_bias,
        merge_bias,
        expand_bias,
        reduce_bias,
        first_gain,
        first_shift,
        second_gain,
        second_shift,
    )
    widths = [values.shape[1] for values in small]
    starts = [sum(widths[:at]) for at in range(len(widths))]
    packed = jnp.concatenate(small, axis=1).astype(bf16)
    gathered = lax.all_gather(packed, BLOCKS)
    gathered = gathered.reshape(4, 4, 3, -1).transpose(0, 2, 1, 3).reshape(12, 4, -1).astype(f32)
    vectors = [
        gathered[:, :, start : start + width].reshape(12, 4 * width)
        for start, width in zip(starts, widths)
    ]
    pairs = vectors[0].reshape(12, 2, HD)
    mixed_bias = jnp.stack([pairs[:, 0], jnp.zeros_like(pairs[:, 0]), pairs[:, 1]], axis=1)
    mixed_bias = widen(mixed_bias.reshape(4, 1, 9 * HD))
    merge_vec, expand_vec, reduce_vec, gain_one, shift_one, gain_two, shift_two = [
        values.reshape(-1) for values in vectors[1:]
    ]

    mixer = lax.all_gather(widen(mixer_weight.astype(bf16)), BLOCKS).reshape(4, D, WIDE)
    merge = lax.all_gather(merge_weight.astype(bf16), BLOCKS).reshape(4, 3 * HD, D)
    merge = jnp.concatenate(
        [merge[:, : 2 * HD], jnp.zeros((4, HD, D), bf16), merge[:, 2 * HD :]], axis=1
    )
    expand = lax.all_gather(expand_weight.astype(bf16), BLOCKS).reshape(4, D, D)
    reduce = lax.all_gather(reduce_weight.astype(bf16), BLOCKS).reshape(4, D, D)

    rows = to_members(inputs, col, member).astype(f32)
    cotan = to_members(cotangent, col, member)
    cotan_wide = cotan.astype(f32)

    normed_one, scaled_one, inverse_one = norm(rows, gain_one, shift_one)
    normed_one = normed_one.astype(bf16)
    mixed = (many(mixer, normed_one, (1,), (1,)).transpose(0, 2, 1) + mixed_bias).astype(bf16)
    slots = to_slots(mixed.reshape(4, 3, ROWS, WIDE), last).reshape(3, KEYS, WIDE)
    outs, sums = attend(slots)
    heads = from_slots(outs.reshape(3, 4, ROWS, 256), last).reshape(4, 3 * ROWS, 256)
    state = rows + many(heads, merge, (0, 2), (0, 1)) + merge_vec
    normed_two, scaled_two, inverse_two = norm(state, gain_two, shift_two)
    normed_two = normed_two.astype(bf16)
    hidden = many(expand, normed_two, (1,), (1,)).transpose(0, 2, 1) + expand_vec.reshape(4, 1, D)
    active, slope = gelu_parts(hidden)
    active = active.astype(bf16)
    result = state + many(active, reduce, (0, 2), (0, 1)) + reduce_vec
    outputs = from_members(result.astype(bf16), col, member)

    grad_reduce_mat = many(active, cotan, (1,), (0,))
    grad_reduce_vec = jnp.sum(cotan_wide, axis=0)
    grad_active = many(reduce, cotan, (2,), (1,)).transpose(0, 2, 1)
    grad_hidden = (grad_active * slope).astype(bf16)
    grad_expand_mat = many(normed_two, grad_hidden, (0,), (1,)).transpose(1, 0, 2)
    grad_expand_vec = jnp.sum(grad_hidden.astype(f32), axis=1)
    back_two, grad_gain_two, grad_shift_two = norm_back(
        many(grad_hidden, expand, (0, 2), (0, 2)), scaled_two, inverse_two, gain_two
    )
    grad_state = cotan_wide + back_two
    grad_branch = grad_state.astype(bf16)
    grad_merge_mat = many(heads, grad_branch, (1,), (0,))
    grad_merge_vec = jnp.sum(grad_branch.astype(f32), axis=0)
    grad_heads = many(merge, grad_branch, (2,), (1,)).transpose(0, 2, 1).astype(bf16)
    grad_slots = to_slots(grad_heads.reshape(4, 3, ROWS, 256), last).reshape(3, KEYS, 256)
    mixed_slots = attend_back(slots, grad_slots, sums)
    grad_mixed = from_slots(mixed_slots.reshape(3, 4, ROWS, WIDE), last)
    grad_mixed = grad_mixed.reshape(4, 3 * ROWS, WIDE)
    grad_mixer_mat = many(normed_one, grad_mixed, (0,), (1,)).transpose(1, 0, 2)
    bias_sums = narrow(jnp.sum(grad_mixed.astype(f32), axis=1)).reshape(12, 3, HD)
    grad_mixer_vec = jnp.stack([bias_sums[:, 0], bias_sums[:, 2]], axis=1)
    back_one, grad_gain_one, grad_shift_one = norm_back(
        many(grad_mixed, mixer, (0, 2), (0, 2)), scaled_one, inverse_one, gain_one
    )
    input_grad = from_members((grad_state + back_one).astype(bf16), col, member).astype(f32)

    def scatter(values):
        blocks = values.astype(bf16).reshape(16, -1, values.shape[-1])
        return lax.psum_scatter(blocks, BLOCKS, scatter_dimension=0, tiled=False)

    grad_merge_mat = jnp.concatenate(
        [grad_merge_mat[:, : 2 * HD], grad_merge_mat[:, 3 * HD :]], axis=1
    )
    parts = [
        scatter(grad_reduce_mat),
        scatter(grad_expand_mat),
        scatter(grad_merge_mat),
        scatter(grad_mixer_mat),
    ]
    part_reduce, part_expand, part_merge, part_mixer = [
        lax.psum(part.astype(f32), "dp") for part in parts
    ]
    totals = (
        grad_mixer_vec,
        grad_merge_vec,
        grad_expand_vec,
        grad_reduce_vec,
        grad_gain_one,
        grad_shift_one,
        grad_gain_two,
        grad_shift_two,
    )
    sizes = [values.size for values in totals]
    joined = lax.psum(
        jnp.concatenate([values.reshape(-1) for values in totals]), ("dp", "row", "col")
    )
    shares = []
    for at, width in enumerate(widths):
        start = sum(sizes[:at])
        whole = joined[start : start + sizes[at]].reshape(12, 4 * width)
        shares.append(lax.dynamic_slice(whole, (3 * col, width * row), (3, width)))
    return (
        outputs,
        input_grad,
        narrow(part_mixer),
        shares[0],
        part_merge,
        shares[1],
        part_expand,
        shares[2],
        part_reduce,
        shares[3],
        shares[4],
        shares[5],
        shares[6],
        shares[7],
    )


def solution(mesh):
    rows = P(("dp", "row"), "col", None)
    square = P("row", "col")
    flat = P(("col", "row"), None)
    small = P("col", "row")
    weights = (square, small, flat, small, square, small, flat, small, small, small, small, small)
    return jax.shard_map(
        body,
        mesh=mesh,
        in_specs=(rows,) + weights + (rows,),
        out_specs=(rows, rows) + weights,
        check_vma=False,
    )
```
